256 devices in a mesh: tok: 32 (over z, y), feat: 8 (over x, core).
Axes of the slice: x: 4, y: 4, z: 8, core: 2. Of those that a mesh axis runs over, the one named last changes fastest.
Arguments:
- activations: bfloat16 [49152, 8192], P('tok', 'feat'), as said below
- start_basis: float32 [32, 8192], P(None, 'feat'), may hold values from -6 to 6
Outputs:
- scores: float32 [49152], P('tok')
- basis: float32 [32, 8192], P(None, 'feat')
The draws below stay inside these ranges and needn't reach their ends.
Inputs may be any that keep to these rules, and one draw needn't show every extreme that they name: `activations`: token rows carry a feature offset whose size varies along the rows, on top of independent entries.
All inputs are finite; a program needn't handle non-finite values.
Results may differ from the reference program's by a relative error of at most 0.0048.
Values may be sent and summed in bfloat16 or wider, within the bound.
A program may use at most 64 MiB of HBM per device.

```python
import jax
import jax.numpy as jnp
from jax import lax

D = 8192
K = 32
ITERS = 4
TOK_DEV = 1536
ROWS = 49152
N_TOK = 32


def draw_activations(key, part):
    key_noise = jax.random.fold_in(key, 11)
    key_offset = jax.random.fold_in(key, 12)
    offset = jax.random.uniform(key_offset, (D,), jnp.float32, -0.1, 0.1)
    position = jnp.arange(ROWS, dtype=jnp.float32) / (ROWS - 1)
    ramp = jnp.exp(2.3025851 * position)
    noise = jax.random.normal(key_noise, (ROWS, D), jnp.float32)
    return (noise + ramp[:, None] * offset[None, :]).astype(jnp.bfloat16)


def shard_levels(key, dims, pieces, smallest, top_value):
    level, own = 1.0, jax.random.fold_in(key, 6)
    for dim, shards_of in pieces:
        draws = jnp.exp(jax.random.uniform(jax.random.fold_in(own, dim), (shards_of,), jnp.float32, smallest / len(pieces), top_value / len(pieces)))
        level = level * jnp.repeat(draws, dims[dim] // shards_of).reshape([-1 if axis == dim else 1 for axis in range(len(dims))])
    return level


def gaussian(key, extent, deviation, bound, pieces=(), held_as=jnp.bfloat16):
    entries = deviation * jax.random.normal(key, extent, jnp.float32)
    if pieces:
        entries = entries * shard_levels(key, extent, pieces, -0.22, 0.18)
    return jnp.clip(entries, -bound, bound).astype(held_as)


def setup_inputs(seed: int = 0) -> dict:
    streams_of = jax.random.split(jax.random.key(seed), 3)
    activations = draw_activations(jax.random.fold_in(streams_of[2], 71), 0)
    start_basis = gaussian(streams_of[1], (K, D), 1.0, 6.0, ((1, 8),), jnp.float32)
    return {"activations": activations, "start_basis": start_basis}


def project(activations, vectors, mean):
    shift = jnp.dot(vectors.astype(jnp.float32), mean, precision=lax.Precision.HIGHEST)
    blocks = activations.reshape(N_TOK, TOK_DEV, D)

    def single(block):
        product = lax.dot_general(vectors.astype(jnp.float32), block.astype(jnp.float32), (((1,), (1,)), ((), ())), preferred_element_type=jnp.float32)
        return product - shift[:, None]
    return lax.map(single, blocks)

def image_of(activations, weights, mean):
    blocks = activations.reshape(N_TOK, TOK_DEV, D)

    def accumulate(total, pair):
        block, weight_block = pair
        term = jnp.dot(weight_block.astype(jnp.float32), block.astype(jnp.float32), preferred_element_type=jnp.float32)
        counts = jnp.sum(weight_block.astype(jnp.float32), axis=1)
        return (total + term - counts[:, None] * mean[None, :], None)
    total, _ = lax.scan(accumulate, jnp.zeros((K, D), jnp.float32), (blocks, weights))
    return total

def reference(activations, start_basis):
    mean = jnp.sum(activations, axis=0, dtype=jnp.float32) / ROWS
    basis = start_basis
    for step in range(ITERS):
        vectors = basis.astype(jnp.bfloat16)
        projected = project(activations, vectors, mean)
        weights = projected.astype(jnp.bfloat16)
        image = image_of(activations, weights, mean)
        gram = jnp.dot(image, image.T, precision=lax.Precision.HIGHEST)
        lower = jnp.linalg.cholesky(gram)
        basis = jax.scipy.linalg.solve_triangular(lower, image, lower=True)
    projected = project(activations, basis.astype(jnp.bfloat16), mean)
    scores = jnp.mean(projected * projected, axis=1).reshape(ROWS)
    return (scores, basis)
```

```python
import functools

import jax
import jax.numpy as jnp
from jax import lax
from jax.experimental import pallas as pl
from jax.experimental.pallas import tpu as pltpu
from jax.sharding import PartitionSpec as P

ITERS = 4
NY = 4
CORES = 2
LANES = 128
SUB = 8
MESH = pl.DeviceIdType.MESH
HIGHEST = lax.Precision.HIGHEST
NT = (((1,), (1,)), ((), ()))


def far_first(n):
    return sorted(range(n), key=lambda d: -min(d, n - d))


def kernel(nz, nx, acts, start, scores, basis, a, x, xb, pbuf, prec, gbuf, grec, w, img, irec, own, crec, mean,
           sbuf, a_sem, send, recv):
    tok, feat = lax.axis_index("tok"), lax.axis_index("feat")
    n_tok, n_feat = nz * NY, nx * CORES
    z, y = tok // NY, tok % NY
    cx, core = feat // CORES, feat % CORES
    k = x.shape[0]
    rows = a.shape[0]
    per_chip = rows // nx
    base = pl.multiple_of(cx * per_chip + core * 2 * LANES, LANES)
    PS, GS, WS, IS, XS, CS, SS = range(7)

    tok_offsets = [(dz, dy) for dz in far_first(nz) for dy in far_first(NY) if (dz, dy) != (0, 0)]
    feat_offsets = [(dx, dc) for dx in far_first(nx) for dc in range(CORES) if (dx, dc) != (0, 0)]

    def tok_peer(dz, dy):
        return lax.rem(z + dz, nz), lax.rem(y + dy, NY)

    def feat_peer(dx, dc):
        return lax.rem(cx + dx, nx), lax.rem(core + dc, CORES)

    def push(src, dst, which, t, f):
        pltpu.make_async_remote_copy(
            src_ref=src, dst_ref=dst, send_sem=send.at[which], recv_sem=recv.at[which],
            device_id=(t, f), device_id_type=MESH,
        ).start()

    def drain(sem, ref):
        pltpu.make_async_copy(ref, ref, sem).wait()

    load = pltpu.make_async_copy(acts, a, a_sem)
    load.start()
    barrier = pltpu.get_barrier_semaphore()
    for dz, dy in tok_offsets:
        tz, ty = tok_peer(dz, dy)
        pl.semaphore_signal(barrier, inc=1, device_id=(tz * NY + ty, feat), device_id_type=MESH)
    for dx, dc in feat_offsets:
        fx, fc = feat_peer(dx, dc)
        pl.semaphore_signal(barrier, inc=1, device_id=(tok, fx * CORES + fc), device_id_type=MESH)

    lane = lax.broadcasted_iota(jnp.int32, (SUB, LANES), 1)
    sub = lax.broadcasted_iota(jnp.int32, (SUB, LANES), 0)

    def chunk(c):
        return slice(c * LANES, (c + 1) * LANES)

    def tile_at(ref, tz, ty):
        return ref.at[pl.ds(pl.multiple_of(ty * SUB, SUB), SUB), pl.ds(pl.multiple_of(tz * LANES, LANES), LANES)]

    def send_projection(r, shift):
        for dx in far_first(nx):
            ox = lax.rem(cx + dx, nx)
            block = a[pl.ds(pl.multiple_of(ox * per_chip, LANES), per_chip), :]
            p = lax.dot_general(xb[0:r, :], block, NT, preferred_element_type=jnp.float32)
            if r > k:
                p = p[:k] + p[k:]
            if shift is not None:
                p = p - shift
            pbuf[dx] = p
            if dx:
                push(pbuf.at[dx, :, 0:2 * LANES], prec.at[feat], PS, tok, ox * CORES)
                push(pbuf.at[dx, :, 2 * LANES:], prec.at[feat, :, 0:LANES], PS, tok, ox * CORES + 1)
            else:
                @pl.when(core == 0)
                def _():
                    push(pbuf.at[dx, :, 2 * LANES:], prec.at[feat, :, 0:LANES], PS, tok, ox * CORES + 1)
                    prec[feat] = p[:, 0:2 * LANES]

                @pl.when(core == 1)
                def _():
                    push(pbuf.at[dx, :, 0:2 * LANES], prec.at[feat], PS, tok, ox * CORES)
                    prec[feat, :, 0:LANES] = p[:, 2 * LANES:]

    def sum_projection():
        @pl.when(core == 0)
        def _():
            drain(recv.at[PS], prec.at[0:n_feat - 1])

        @pl.when(core == 1)
        def _():
            drain(recv.at[PS], prec.at[0:n_feat - 1, :, 0:LANES])

        total = prec[0]
        for s in range(1, n_feat):
            total = total + prec[s]
        for dx in range(1, nx):
            drain(send.at[PS], pbuf.at[dx])

        @pl.when(core == 0)
        def _():
            drain(send.at[PS], pbuf.at[0, :, 2 * LANES:])

        @pl.when(core == 1)
        def _():
            drain(send.at[PS], pbuf.at[0, :, 0:2 * LANES])

        return total

    def own_columns(ref, r, body):
        @pl.when(core == 0)
        def _():
            body(ref.at[0:r, pl.ds(base, 2 * LANES)], 2 * LANES)

        @pl.when(core == 1)
        def _():
            body(ref.at[0:r, pl.ds(base, LANES)], LANES)

    def gather_columns(ref, r, which, value):
        def share(mine, width):
            mine[...] = value[:, 0:width]
            for dx, dc in feat_offsets:
                fx, fc = feat_peer(dx, dc)
                push(mine, mine, which, tok, fx * CORES + fc)

        own_columns(ref, r, share)

        @pl.when(core == 0)
        def _():
            drain(recv.at[which], ref.at[0:r, 0:rows - 2 * LANES])

        @pl.when(core == 1)
        def _():
            drain(recv.at[which], ref.at[0:r, 0:rows - LANES])

    def sent_columns(ref, r, which):
        def body(mine, width):
            for _ in feat_offsets:
                drain(send.at[which], mine)

        own_columns(ref, r, body)

    def send_gram():
        both = xb[...]
        s = lax.dot_general(both, jnp.concatenate([both, both], axis=0), NT, preferred_element_type=jnp.float32)
        s = s[:k] + s[k:]
        packed = jnp.zeros((SUB, LANES), jnp.float32)
        for g in range(k // SUB):
            part = s[g * SUB:(g + 1) * SUB]
            part = jnp.where(lane < k, part + pltpu.roll(part, LANES - k, 1), 0.0)
            packed = packed + (pltpu.roll(part, g * k, 1) if g else part)
        gbuf[...] = packed
        grec[feat] = packed
        for dx, dc in feat_offsets:
            fx, fc = feat_peer(dx, dc)
            push(gbuf, grec.at[feat], GS, tok, fx * CORES + fc)

    def inverse_factor():
        drain(recv.at[GS], grec.at[0:n_feat - 1])
        packed = grec[0]
        for s in range(1, n_feat):
            packed = packed + grec[s]
        for _ in feat_offsets:
            drain(send.at[GS], gbuf)
        groups = []
        for g in range(k // SUB):
            part = pltpu.roll(packed, LANES - g * k, 1) if g else packed
            groups.append(jnp.where(lane < k, part, jnp.where(lane - k == sub + g * SUB, 1.0, 0.0)))
        m = jnp.concatenate(groups, axis=0)
        row = lax.broadcasted_iota(jnp.int32, (k, 1), 0)
        diag = jnp.ones((k, 1), jnp.float32)
        for j in range(k):
            pivot_row = m[j:j + 1, :]
            pivot = m[j:j + 1, j:j + 1]
            diag = jnp.where(row == j, pivot, diag)
            factor = jnp.where(row > j, m[:, j:j + 1] * (1.0 / pivot), 0.0)
            m = m - factor * pivot_row
        m = m * lax.rsqrt(diag)
        return pltpu.roll(m, LANES - k, 1)[:, 0:k]

    def split():
        v = x[...]
        hi = v.astype(jnp.bfloat16)
        hi32 = hi.astype(jnp.float32)
        lo = (v - hi32).astype(jnp.bfloat16)
        xb[0:k, :] = hi
        xb[k:, :] = lo
        return hi32 + lo.astype(jnp.float32)

    def centred_projection():
        v = split()
        send_gram()
        acc = jnp.zeros((k, LANES), jnp.float32)
        for c in range(nz):
            acc = acc + v[:, chunk(c)] * mean[c:c + 1, :]
        send_projection(2 * k, jnp.sum(acc, axis=1, keepdims=True))
        inv = inverse_factor()
        total = sum_projection()
        return inv, jnp.dot(inv, total, precision=HIGHEST, preferred_element_type=jnp.float32)

    def reduce_image(r):
        weights = w[0:r, :]
        term = jnp.dot(weights, a[...], preferred_element_type=jnp.float32)
        counts = jnp.sum(weights.astype(jnp.float32), axis=1, keepdims=True)
        if r > k:
            term = term[:k] + term[k:]
            counts = counts[:k] + counts[k:]
            drain(recv.at[CS], crec.at[0:n_tok - 1])
            total = crec[0]
            for s in range(1, n_tok):
                total = total + crec[s]
            mean[...] = total / (n_tok * rows)
        for c in range(nz):
            img[:, chunk(c)] = term[:, chunk(c)] - counts * mean[c:c + 1, :]
        for dz, dy in tok_offsets:
            tz, ty = tok_peer(dz, dy)
            push(tile_at(img, tz, ty), irec.at[tok], IS, tz * NY + ty, feat)
        irec[tok] = tile_at(img, z, y)[...]
        drain(recv.at[IS], irec.at[0:n_tok - 1])
        total = irec[0]
        for s in range(1, n_tok):
            total = total + irec[s]
        own[...] = total
        mine = tile_at(x, z, y)
        for dz, dy in tok_offsets:
            tz, ty = tok_peer(dz, dy)
            push(own, mine, XS, tz * NY + ty, feat)
        mine[...] = total
        sent_columns(w, r, WS)
        drain(send.at[IS], irec.at[0:n_tok - 1])
        drain(recv.at[XS], irec.at[0:n_tok - 1])
        drain(send.at[XS], irec.at[0:n_tok - 1])

    xb[0:k, :] = start[...].astype(jnp.bfloat16)
    load.wait()
    sums = jnp.dot(jnp.ones((SUB, rows), jnp.bfloat16), a[...], preferred_element_type=jnp.float32)
    packed_sums = jnp.zeros((SUB, LANES), jnp.float32)
    for c in range(nz):
        packed_sums = jnp.where(sub == c, sums[:, chunk(c)], packed_sums)
    own[...] = packed_sums
    crec[tok] = packed_sums
    pl.semaphore_wait(barrier, n_tok + n_feat - 2)
    for dz, dy in tok_offsets:
        tz, ty = tok_peer(dz, dy)
        push(own, crec.at[tok], CS, tz * NY + ty, feat)
    send_projection(k, None)
    total = sum_projection()
    hi = total.astype(jnp.bfloat16)
    lo = (total - hi.astype(jnp.float32)).astype(jnp.bfloat16)
    gather_columns(w, 2 * k, WS, jnp.concatenate([hi, lo], axis=0))
    drain(send.at[CS], irec.at[0:n_tok - 1])
    reduce_image(2 * k)

    def advance(step, carry):
        _, projected = centred_projection()
        gather_columns(w, k, WS, projected.astype(jnp.bfloat16))
        reduce_image(k)
        return carry

    lax.fori_loop(1, ITERS, advance, 0)
    inv, projected = centred_projection()
    gather_columns(sbuf, 1, SS, jnp.mean(projected * projected, axis=0, keepdims=True))
    basis[...] = jnp.dot(inv, x[...], precision=HIGHEST, preferred_element_type=jnp.float32)
    sent_columns(sbuf, 1, SS)
    scores[...] = sbuf[...]


def solution(mesh):
    n_tok, n_feat = mesh.shape["tok"], mesh.shape["feat"]
    nz, nx = n_tok // NY, n_feat // CORES

    def on_device(activations, start_basis):
        rows, cols = activations.shape
        k = start_basis.shape[0]
        vmem = pl.BlockSpec(memory_space=pltpu.VMEM)
        scores, basis = pl.pallas_call(
            functools.partial(kernel, nz, nx),
            out_shape=(jax.ShapeDtypeStruct((1, rows), jnp.float32), jax.ShapeDtypeStruct((k, cols), jnp.float32)),
            in_specs=[pl.BlockSpec(memory_space=pl.ANY), vmem],
            out_specs=(vmem, vmem),
            scratch_shapes=[
                pltpu.VMEM((rows, cols), jnp.bfloat16),
                pltpu.VMEM((k, cols), jnp.float32),
                pltpu.VMEM((2 * k, cols), jnp.bfloat16),
                pltpu.VMEM((nx, k, rows // nx), jnp.float32),
                pltpu.VMEM((n_feat, k, 2 * LANES), jnp.float32),
                pltpu.VMEM((SUB, LANES), jnp.float32),
                pltpu.VMEM((n_feat, SUB, LANES), jnp.float32),
                pltpu.VMEM((2 * k, rows), jnp.bfloat16),
                pltpu.VMEM((k, cols), jnp.float32),
                pltpu.VMEM((n_tok, SUB, LANES), jnp.float32),
                pltpu.VMEM((SUB, LANES), jnp.float32),
                pltpu.VMEM((n_tok, SUB, LANES), jnp.float32),
                pltpu.VMEM((SUB, LANES), jnp.float32),
                pltpu.VMEM((1, rows), jnp.float32),
                pltpu.SemaphoreType.DMA,
                pltpu.SemaphoreType.DMA((7,)),
                pltpu.SemaphoreType.DMA((7,)),
            ],
            compiler_params=pltpu.CompilerParams(collective_id=0, has_side_effects=True),
        )(activations, start_basis)
        return scores[0], basis

    return jax.shard_map(
        on_device, mesh=mesh, in_specs=(P("tok", "feat"), P(None, "feat")),
        out_specs=(P("tok"), P(None, "feat")), check_vma=False,
    )
```

```python
import functools

import jax
import jax.numpy as jnp
from jax import lax
from jax.experimental import pallas as pl
from jax.experimental.pallas import tpu as pltpu
from jax.sharding import PartitionSpec as P

ITERS = 4
NY = 4
CORES = 2
LANES = 128
SUB = 8
MESH = pl.DeviceIdType.MESH
HIGHEST = lax.Precision.HIGHEST
NT = (((1,), (1,)), ((), ()))


def far_first(n):
    return sorted(range(n), key=lambda d: -min(d, n - d))


def tree_sum(terms):
    terms = list(terms)
    while len(terms) > 1:
        terms = [sum(terms[i + 1:i + 2], terms[i]) for i in range(0, len(terms), 2)]
    return terms[0]


def kernel(nz, nx, acts, start, scores, basis, a, x, xb, pbuf, prec, gbuf, grec, w, img, irec, own, crec, mean,
           sbuf, ibuf, a_sem, send, recv, precv):
    tok, feat = lax.axis_index("tok"), lax.axis_index("feat")
    n_tok, n_feat = nz * NY, nx * CORES
    z, y = tok // NY, tok % NY
    cx, core = feat // CORES, feat % CORES
    owner = cx * CORES + 1
    other = cx * CORES + 1 - core
    k = x.shape[0]
    rows = a.shape[0]
    width = rows // nx
    mine = pl.ds(pl.multiple_of(cx * width, LANES), width)
    PS, GS, WS, IS, XS, CS, SS, BS = range(8)

    tok_offsets = sorted(((dz, dy) for dz in range(nz) for dy in range(NY) if (dz, dy) != (0, 0)),
                         key=lambda o: -min(o[0], nz - o[0]) - min(o[1], NY - o[1]))

    def tok_peer(dz, dy):
        return lax.rem(z + dz, nz) * NY + lax.rem(y + dy, NY)

    def chip(dx):
        return lax.rem(cx + dx, nx)

    def push(src, dst, which, t, f, arrived=None):
        pltpu.make_async_remote_copy(
            src_ref=src, dst_ref=dst, send_sem=send.at[which],
            recv_sem=recv.at[which] if arrived is None else arrived,
            device_id=(t, f), device_id_type=MESH,
        ).start()

    def drain(sem, ref):
        pltpu.make_async_copy(ref, ref, sem).wait()

    def on_core(c):
        return pl.when(core == c)

    load = pltpu.make_async_copy(acts, a, a_sem)
    load.start()
    barrier = pltpu.get_barrier_semaphore()

    def greet(t, f):
        pl.semaphore_signal(barrier, inc=1, device_id=(t, f), device_id_type=MESH)

    for dz, dy in tok_offsets:
        greet(tok_peer(dz, dy), feat)
        greet(tok_peer(dz, dy), other)
    for dx in far_first(nx):
        greet(tok, chip(dx) * CORES + 1 - core)
        if dx:
            greet(tok, chip(dx) * CORES + core)

    lane = lax.broadcasted_iota(jnp.int32, (SUB, LANES), 1)
    sub = lax.broadcasted_iota(jnp.int32, (SUB, LANES), 0)

    def chunk(c):
        return slice(c * LANES, (c + 1) * LANES)

    def tile_at(ref, tz, ty):
        return ref.at[pl.ds(pl.multiple_of(ty * SUB, SUB), SUB), pl.ds(pl.multiple_of(tz * LANES, LANES), LANES)]

    def send_projection(r, shift):
        for dx in far_first(nx):
            to = chip(dx)
            block = a[pl.ds(pl.multiple_of(to * width, LANES), width), :]
            p = lax.dot_general(xb[0:r, :], block, NT, preferred_element_type=jnp.float32)
            if r > k:
                p = p[:k] + p[k:]
            if shift is not None:
                p = p - shift
            if dx:
                pbuf[dx] = p
                push(pbuf.at[dx], prec.at[dx * CORES + core], PS, tok, to * CORES + 1, precv.at[dx])
            else:
                @on_core(0)
                def _():
                    pbuf[0] = p
                    push(pbuf.at[0], prec.at[0], PS, tok, owner, precv.at[0])

                @on_core(1)
                def _():
                    prec[1] = p

    def sum_projection():
        drain(precv.at[0], prec.at[0])
        total = prec[0] + prec[1]
        for dx in reversed(far_first(nx)[:-1]):
            drain(precv.at[dx], prec.at[0:CORES])
            total = total + (prec[dx * CORES] + prec[dx * CORES + 1])
        return total

    def sent_projection():
        @on_core(0)
        def _():
            drain(send.at[PS], pbuf)

        @on_core(1)
        def _():
            drain(send.at[PS], pbuf.at[1:])

    def share_columns(ref, r, which, value):
        part = ref.at[0:r, mine]
        part[...] = value
        for dx in far_first(nx):
            push(part, part, which, tok, chip(dx) * CORES)
            if dx:
                push(part, part, which, tok, chip(dx) * CORES + 1)

    def await_columns(ref, r, which):
        @on_core(0)
        def _():
            drain(recv.at[which], ref.at[0:r])

        @on_core(1)
        def _():
            drain(recv.at[which], ref.at[0:r, 0:rows - width])

    def sent_columns(ref, r, which):
        @on_core(1)
        def _():
            drain(send.at[which], ref.at[0:r])
            drain(send.at[which], ref.at[0:r, 0:rows - width])

    def send_gram():
        both = xb[...]
        s = lax.dot_general(both, jnp.concatenate([both, both], axis=0), NT, preferred_element_type=jnp.float32)
        s = s[:k] + s[k:]
        packed = jnp.zeros((SUB, LANES), jnp.float32)
        for g in range(k // SUB):
            part = s[g * SUB:(g + 1) * SUB]
            part = jnp.where(lane < k, part + pltpu.roll(part, LANES - k, 1), 0.0)
            packed = packed + (pltpu.roll(part, g * k, 1) if g else part)
        gbuf[...] = packed
        for dx in far_first(nx)[:-1]:
            push(gbuf, grec.at[feat], GS, tok, chip(dx) * CORES + 1)

        @on_core(0)
        def _():
            push(gbuf, grec.at[feat], GS, tok, owner)

        @on_core(1)
        def _():
            grec[feat] = packed

    def sent_gram():
        for _ in range(nx - 1):
            drain(send.at[GS], gbuf)

        @on_core(0)
        def _():
            drain(send.at[GS], gbuf)

    def inverse_factor():
        drain(recv.at[GS], grec.at[0:n_feat - 1])
        packed = tree_sum(grec[s] for s in range(n_feat))
        groups = []
        for g in range(k // SUB):
            part = pltpu.roll(packed, LANES - g * k, 1) if g else packed
            groups.append(jnp.where(lane < k, part, jnp.where(lane - k == sub + g * SUB, 1.0, 0.0)))
        for j in range(k):
            first, r = j // SUB, j % SUB
            pivot = groups[first][r:r + 1, :]
            scaled = pivot * (1.0 / pivot[:, j:j + 1])
            for g in range(first, k // SUB):
                factor = groups[g][:, j:j + 1]
                if g == first:
                    factor = jnp.where(sub[:, 0:1] > r, factor, 0.0)
                groups[g] = groups[g] - factor * scaled
        for g in range(k // SUB):
            diag = jnp.sum(jnp.where(lane == sub + g * SUB, groups[g], 0.0), axis=1, keepdims=True)
            groups[g] = pltpu.roll(groups[g] * lax.rsqrt(diag), LANES - k, 1)
        return jnp.concatenate(groups, axis=0)

    def split():
        v = x[...]
        hi = v.astype(jnp.bfloat16)
        hi32 = hi.astype(jnp.float32)
        lo = (v - hi32).astype(jnp.bfloat16)
        xb[0:k, :] = hi
        xb[k:, :] = lo
        return hi32 + lo.astype(jnp.float32)

    def send_centred():
        v = split()
        send_gram()
        acc = jnp.zeros((k, LANES), jnp.float32)
        for c in range(nz):
            acc = acc + v[:, chunk(c)] * mean[c:c + 1, :]
        send_projection(2 * k, jnp.sum(acc, axis=1, keepdims=True))

    def normalised(inv):
        return jnp.dot(inv[:, 0:k], sum_projection(), precision=HIGHEST, preferred_element_type=jnp.float32)

    def reduce_image(r):
        await_columns(w, r, WS)
        weights = w[0:r, :]
        counts = jnp.sum(weights.astype(jnp.float32), axis=1, keepdims=True)
        if r > k:
            counts = counts[:k] + counts[k:]
            drain(recv.at[CS], crec.at[0:n_tok - 1])
            mean[...] = tree_sum(crec[s] for s in range(n_tok)) / (n_tok * rows)
        slot = irec.at[core * n_tok + tok]
        pairs = nz // 2
        for dg in far_first(pairs):
            g = lax.rem(z // 2 + dg, pairs)
            columns = pl.ds(pl.multiple_of(g * 2 * LANES, 2 * LANES), 2 * LANES)
            term = jnp.dot(weights, a[:, columns], preferred_element_type=jnp.float32)
            if r > k:
                term = term[:k] + term[k:]
            for e in range(2):
                tz = g * 2 + e
                tile_column = pl.ds(pl.multiple_of(tz * LANES, LANES), LANES)
                img[:, tile_column] = term[:, chunk(e)] - counts * mean[pl.ds(tz, 1), :]
            for dy in far_first(NY):
                ty = lax.rem(y + dy, NY)
                if dg or dy:
                    for e in range(2):
                        push(tile_at(img, g * 2 + e, ty), slot, IS, (g * 2 + e) * NY + ty, owner)
                else:
                    tz = g * 2 + 1 - z % 2
                    push(tile_at(img, tz, ty), slot, IS, tz * NY + ty, owner)

                    @on_core(0)
                    def _():
                        push(tile_at(img, z, y), slot, IS, tok, owner)

                    @on_core(1)
                    def _():
                        irec[n_tok + tok] = tile_at(img, z, y)[...]

        tile = tile_at(x, z, y)

        @on_core(0)
        def _():
            drain(recv.at[XS], irec.at[0:n_tok])

        @on_core(1)
        def _():
            drain(recv.at[IS], irec.at[0:2 * n_tok - 1])
            for c in range(CORES):
                own[c] = tree_sum(irec[c * n_tok + s] for s in range(n_tok))
            for dz, dy in tok_offsets:
                for c in range(CORES):
                    push(own.at[c], tile, XS, tok_peer(dz, dy), cx * CORES + c)
            push(own.at[0], tile, XS, tok, cx * CORES)
            tile[...] = own[1]
            drain(recv.at[XS], irec.at[0:n_tok - 1])

    def sent_image():
        @on_core(0)
        def _():
            drain(send.at[IS], irec.at[0:n_tok])

        @on_core(1)
        def _():
            drain(send.at[IS], irec.at[0:n_tok - 1])
            drain(send.at[XS], irec.at[0:2 * n_tok - 1])

    xb[0:k, :] = start[...].astype(jnp.bfloat16)
    load.wait()
    sums = jnp.dot(jnp.ones((SUB, rows), jnp.bfloat16), a[...], preferred_element_type=jnp.float32)
    packed_sums = jnp.zeros((SUB, LANES), jnp.float32)
    for c in range(nz):
        packed_sums = jnp.where(sub == c, sums[:, chunk(c)], packed_sums)
    gbuf[...] = packed_sums
    crec[tok] = packed_sums
    pl.semaphore_wait(barrier, 2 * (n_tok - 1) + n_feat - 1)
    send_projection(k, None)
    for dz, dy in tok_offsets:
        push(gbuf, crec.at[tok], CS, tok_peer(dz, dy), feat)

    @on_core(1)
    def _():
        total = sum_projection()
        hi = total.astype(jnp.bfloat16)
        lo = (total - hi.astype(jnp.float32)).astype(jnp.bfloat16)
        share_columns(w, 2 * k, WS, jnp.concatenate([hi, lo], axis=0))

    drain(send.at[CS], irec.at[0:n_tok - 1])
    sent_projection()
    reduce_image(2 * k)
    sent_columns(w, 2 * k, WS)

    def advance(step, carry):
        send_centred()
        sent_image()

        @on_core(1)
        def _():
            inv = inverse_factor()
            share_columns(w, k, WS, normalised(inv).astype(jnp.bfloat16))

        sent_projection()
        sent_gram()
        reduce_image(k)
        sent_columns(w, k, WS)
        return carry

    lax.fori_loop(1, ITERS, advance, 0)
    send_centred()
    sent_image()

    @on_core(1)
    def _():
        inv = inverse_factor()
        ibuf[...] = inv
        push(ibuf, ibuf, BS, tok, cx * CORES)
        projected = normalised(inv)
        share_columns(sbuf, 1, SS, jnp.mean(projected * projected, axis=0, keepdims=True))

    @on_core(0)
    def _():
        drain(recv.at[BS], ibuf)

    basis[...] = jnp.dot(ibuf[:, 0:k], x[...], precision=HIGHEST, preferred_element_type=jnp.float32)
    sent_projection()
    sent_gram()

    @on_core(1)
    def _():
        drain(send.at[BS], ibuf)

    sent_columns(sbuf, 1, SS)
    await_columns(sbuf, 1, SS)
    scores[...] = sbuf[...]


def finish(scores, basis, scores_out, basis_out):
    scores_out[...] = scores[0]
    basis_out[...] = basis[...]


def solution(mesh):
    n_tok, n_feat = mesh.shape["tok"], mesh.shape["feat"]
    nz, nx = n_tok // NY, n_feat // CORES

    def on_device(activations, start_basis):
        rows, cols = activations.shape
        k = start_basis.shape[0]
        vmem = pl.BlockSpec(memory_space=pltpu.VMEM)
        scores, basis = pl.pallas_call(
            functools.partial(kernel, nz, nx),
            out_shape=(jax.ShapeDtypeStruct((1, rows), jnp.float32), jax.ShapeDtypeStruct((k, cols), jnp.float32)),
            in_specs=[pl.BlockSpec(memory_space=pl.ANY), vmem],
            out_specs=(vmem, vmem),
            scratch_shapes=[
                pltpu.VMEM((rows, cols), jnp.bfloat16),
                pltpu.VMEM((k, cols), jnp.float32),
                pltpu.VMEM((2 * k, cols), jnp.bfloat16),
                pltpu.VMEM((nx, k, rows // nx), jnp.float32),
                pltpu.VMEM((n_feat, k, rows // nx), jnp.float32),
                pltpu.VMEM((SUB, LANES), jnp.float32),
                pltpu.VMEM((n_feat, SUB, LANES), jnp.float32),
                pltpu.VMEM((2 * k, rows), jnp.bfloat16),
                pltpu.VMEM((k, cols), jnp.float32),
                pltpu.VMEM((2 * n_tok, SUB, LANES), jnp.float32),
                pltpu.VMEM((CORES, SUB, LANES), jnp.float32),
                pltpu.VMEM((n_tok, SUB, LANES), jnp.float32),
                pltpu.VMEM((SUB, LANES), jnp.float32),
                pltpu.VMEM((1, rows), jnp.float32),
                pltpu.VMEM((k, LANES), jnp.float32),
                pltpu.SemaphoreType.DMA,
                pltpu.SemaphoreType.DMA((8,)),
                pltpu.SemaphoreType.DMA((8,)),
                pltpu.SemaphoreType.DMA((nx,)),
            ],
            compiler_params=pltpu.CompilerParams(collective_id=0, has_side_effects=True),
        )(activations, start_basis)
        return pl.pallas_call(
            finish,
            out_shape=(jax.ShapeDtypeStruct((rows,), jnp.float32), jax.ShapeDtypeStruct((k, cols), jnp.float32)),
            in_specs=[vmem, vmem],
            out_specs=(vmem, vmem),
        )(scores, basis)

    return jax.shard_map(
        on_device, mesh=mesh, in_specs=(P("tok", "feat"), P(None, "feat")),
        out_specs=(P("tok"), P(None, "feat")), check_vma=False,
    )
```

```python
import functools

import jax
import jax.numpy as jnp
from jax import lax
from jax.experimental import pallas as pl
from jax.experimental.pallas import tpu as pltpu
from jax.sharding import PartitionSpec as P

ITERS = 4
NY = 4
CORES = 2
LANES = 128
SUB = 8
MESH = pl.DeviceIdType.MESH
HIGHEST = lax.Precision.HIGHEST
NT = (((1,), (1,)), ((), ()))


def far_first(n):
    return sorted(range(n), key=lambda d: -min(d, n - d))


def tree_sum(terms):
    terms = list(terms)
    while len(terms) > 1:
        terms = [sum(terms[i + 1:i + 2], terms[i]) for i in range(0, len(terms), 2)]
    return terms[0]


def wide(v):
    return jnp.broadcast_to(v, (SUB, LANES))


def kernel(nz, nx, acts, start, scores, basis, a, x, xb, pbuf, prec, gbuf, grec, w, img, irec, own, crec, mean,
           sbuf, ibuf, a_sem, send, recv, precv):
    tok, feat = lax.axis_index("tok"), lax.axis_index("feat")
    n_tok, n_feat = nz * NY, nx * CORES
    z, y = tok // NY, tok % NY
    cx, core = feat // CORES, feat % CORES
    owner = cx * CORES + 1
    k = x.shape[0]
    rows = a.shape[0]
    width = rows // nx
    mine = pl.ds(pl.multiple_of(cx * width, LANES), width)
    PS, GS, WS, IS, XS, CS, SS, BS = range(8)

    tok_offsets = sorted(((dz, dy) for dz in range(nz) for dy in range(NY) if (dz, dy) != (0, 0)),
                         key=lambda o: -min(o[0], nz - o[0]) - min(o[1], NY - o[1]))

    def tok_peer(dz, dy):
        return lax.rem(z + dz, nz) * NY + lax.rem(y + dy, NY)

    def chip(dx):
        return lax.rem(cx + dx, nx)

    def push(src, dst, which, t, f, arrived=None):
        pltpu.make_async_remote_copy(
            src_ref=src, dst_ref=dst, send_sem=send.at[which],
            recv_sem=recv.at[which] if arrived is None else arrived,
            device_id=(t, f), device_id_type=MESH,
        ).start()

    def drain(sem, ref):
        pltpu.make_async_copy(ref, ref, sem).wait()

    def on_core(c):
        return pl.when(core == c)

    first = pltpu.make_async_copy(start, img, a_sem.at[0])
    first.start()
    load = pltpu.make_async_copy(acts, a, a_sem.at[1])
    load.start()
    barrier = pltpu.get_barrier_semaphore()

    def greet(t, f):
        pl.semaphore_signal(barrier, inc=1, device_id=(t, f), device_id_type=MESH)

    for dz, dy in tok_offsets:
        greet(tok_peer(dz, dy), feat)
    for dx in far_first(nx):
        greet(tok, chip(dx) * CORES + 1 - core)
        if dx:
            greet(tok, chip(dx) * CORES + core)

    lane = lax.broadcasted_iota(jnp.int32, (SUB, LANES), 1)
    sub = lax.broadcasted_iota(jnp.int32, (SUB, LANES), 0)

    def chunk(c):
        return slice(c * LANES, (c + 1) * LANES)

    def tile_at(ref, tz, ty):
        return ref.at[pl.ds(pl.multiple_of(ty * SUB, SUB), SUB), pl.ds(pl.multiple_of(tz * LANES, LANES), LANES)]

    def send_projection(r, shift):
        for dx in far_first(nx):
            to = chip(dx)
            block = a[pl.ds(pl.multiple_of(to * width, LANES), width), :]
            p = lax.dot_general(xb[0:r, :], block, NT, preferred_element_type=jnp.float32)
            if r > k:
                p = p[:k] + p[k:]
            if shift is not None:
                p = p - shift
            if shift is None:
                pbuf[dx] = p
                continue
            if dx:
                pbuf[dx] = p
                push(pbuf.at[dx], prec.at[dx * CORES + core], PS, tok, to * CORES + 1, precv.at[dx])
            else:
                @on_core(0)
                def _():
                    pbuf[0] = p
                    push(pbuf.at[0], prec.at[0], PS, tok, owner, precv.at[0])

                @on_core(1)
                def _():
                    prec[1] = p

    def sum_projection():
        drain(precv.at[0], prec.at[0])
        total = prec[0] + prec[1]
        for dx in reversed(far_first(nx)[:-1]):
            drain(precv.at[dx], prec.at[0:CORES])
            total = total + (prec[dx * CORES] + prec[dx * CORES + 1])
        return total

    def sent_projection():
        @on_core(0)
        def _():
            drain(send.at[PS], pbuf)

        @on_core(1)
        def _():
            drain(send.at[PS], pbuf.at[1:])

    def share_columns(ref, r, which, value):
        part = ref.at[0:r, mine]
        part[...] = value
        for dx in far_first(nx):
            push(part, part, which, tok, chip(dx) * CORES)
            if dx:
                push(part, part, which, tok, chip(dx) * CORES + 1)

    def await_columns(ref, r, which):
        @on_core(0)
        def _():
            drain(recv.at[which], ref.at[0:r])

        @on_core(1)
        def _():
            drain(recv.at[which], ref.at[0:r, 0:rows - width])

    def sent_columns(ref, r, which):
        @on_core(1)
        def _():
            drain(send.at[which], ref.at[0:r])
            drain(send.at[which], ref.at[0:r, 0:rows - width])

    def send_gram():
        both = xb[...]
        s = lax.dot_general(both, jnp.concatenate([both, both], axis=0), NT, preferred_element_type=jnp.float32)
        s = s[:k] + s[k:]
        packed = jnp.zeros((SUB, LANES), jnp.float32)
        for g in range(k // SUB):
            part = s[g * SUB:(g + 1) * SUB]
            part = jnp.where(lane < k, part + pltpu.roll(part, LANES - k, 1), 0.0)
            packed = packed + (pltpu.roll(part, g * k, 1) if g else part)
        gbuf[...] = packed
        for dx in far_first(nx)[:-1]:
            push(gbuf, grec.at[feat], GS, tok, chip(dx) * CORES + 1)

        @on_core(0)
        def _():
            push(gbuf, grec.at[feat], GS, tok, owner)

        @on_core(1)
        def _():
            grec[feat] = packed

    def sent_gram():
        for _ in range(nx - 1):
            drain(send.at[GS], gbuf)

        @on_core(0)
        def _():
            drain(send.at[GS], gbuf)

    def inverse_factor():
        drain(recv.at[GS], grec.at[0:n_feat - 1])
        packed = tree_sum(grec[s] for s in range(n_feat))
        groups = []
        for g in range(k // SUB):
            part = pltpu.roll(packed, LANES - g * k, 1) if g else packed
            groups.append(jnp.where(lane < k, part, jnp.where(lane - k == sub + g * SUB, 1.0, 0.0)))
        factor = []
        for b in range(k // SUB):
            column = [[wide(g[:, b * SUB + c:b * SUB + c + 1]) for g in groups[b:]] for c in range(SUB)]
            done = jnp.zeros((SUB, LANES), jnp.float32)
            for r in range(SUB):
                pivot = wide(column[r][0][r:r + 1, :])
                inverse = 1.0 / pivot
                pivot_row = wide(groups[b][r:r + 1, :])
                done = jnp.where(sub == r, pivot_row * lax.rsqrt(pivot), done)
                below = [jnp.where(sub > r, column[r][0], 0.0)] + column[r][1:]
                for c in range(r + 1, SUB):
                    scale = wide(column[c][0][r:r + 1, :]) * inverse
                    column[c] = [v - u * scale for v, u in zip(column[c], below)]
                scaled = pivot_row * inverse
                groups[b:] = [g - u * scaled for g, u in zip(groups[b:], below)]
            factor.append(pltpu.roll(done, LANES - k, 1))
        return jnp.concatenate(factor, axis=0)

    def split():
        v = x[...]
        hi = v.astype(jnp.bfloat16)
        hi32 = hi.astype(jnp.float32)
        lo = (v - hi32).astype(jnp.bfloat16)
        xb[0:k, :] = hi
        xb[k:, :] = lo
        return hi32 + lo.astype(jnp.float32)

    def send_centred():
        v = split()
        send_gram()
        acc = jnp.zeros((k, LANES), jnp.float32)
        for c in range(nz):
            acc = acc + v[:, chunk(c)] * mean[c:c + 1, :]
        send_projection(2 * k, jnp.sum(acc, axis=1, keepdims=True))

    def normalised(inv):
        return jnp.dot(inv[:, 0:k], sum_projection(), precision=HIGHEST, preferred_element_type=jnp.float32)

    def reduce_image(r):
        await_columns(w, r, WS)
        weights = w[0:r, :]
        counts = jnp.sum(weights.astype(jnp.float32), axis=1, keepdims=True)
        if r > k:
            counts = counts[:k] + counts[k:]
            drain(recv.at[CS], crec.at[0:n_tok - 1])
            mean[...] = tree_sum(crec[s] for s in range(n_tok)) / (n_tok * rows)
        pairs = nz // 2
        for dg in far_first(pairs):
            g = lax.rem(z // 2 + dg, pairs)
            columns = pl.ds(pl.multiple_of(g * 2 * LANES, 2 * LANES), 2 * LANES)
            term = jnp.dot(weights, a[:, columns], preferred_element_type=jnp.float32)
            if r > k:
                term = term[:k] + term[k:]
            for e in range(2):
                tz = g * 2 + e
                tile_column = pl.ds(pl.multiple_of(tz * LANES, LANES), LANES)
                img[:, tile_column] = term[:, chunk(e)] - counts * mean[pl.ds(tz, 1), :]
            for dy in far_first(NY):
                ty = lax.rem(y + dy, NY)
                for e in range(1 if dg == 0 and dy == 0 else 0, 2):
                    tz = g * 2 + (lax.rem(z + e, 2) if dg == 0 else e)
                    push(tile_at(img, tz, ty), irec.at[tok], IS, tz * NY + ty, feat)
        irec[tok] = tile_at(img, z, y)[...]
        drain(recv.at[IS], irec.at[0:n_tok - 1])
        own[0] = tree_sum(irec[s] for s in range(n_tok))
        tile = tile_at(x, z, y)
        for dz, dy in tok_offsets:
            push(own.at[0], tile, XS, tok_peer(dz, dy), feat)
        tile[...] = own[0]
        drain(recv.at[XS], irec.at[0:n_tok - 1])

    def sent_image():
        drain(send.at[IS], irec.at[0:n_tok - 1])
        drain(send.at[XS], irec.at[0:n_tok - 1])

    first.wait()
    xb[0:k, :] = img[...].astype(jnp.bfloat16)
    load.wait()
    sums = jnp.dot(jnp.ones((SUB, rows), jnp.bfloat16), a[...], preferred_element_type=jnp.float32)
    packed_sums = jnp.zeros((SUB, LANES), jnp.float32)
    for c in range(nz):
        packed_sums = jnp.where(sub == c, sums[:, chunk(c)], packed_sums)
    gbuf[...] = packed_sums
    crec[tok] = packed_sums
    send_projection(k, None)
    pl.semaphore_wait(barrier, n_tok + n_feat - 2)
    for dx in far_first(nx)[:-1]:
        push(pbuf.at[dx], prec.at[dx * CORES + core], PS, tok, chip(dx) * CORES + 1, precv.at[dx])

    @on_core(0)
    def _():
        push(pbuf.at[0], prec.at[0], PS, tok, owner, precv.at[0])

    @on_core(1)
    def _():
        prec[1] = pbuf[0]

    for dz, dy in tok_offsets:
        push(gbuf, crec.at[tok], CS, tok_peer(dz, dy), feat)

    @on_core(1)
    def _():
        total = sum_projection()
        hi = total.astype(jnp.bfloat16)
        lo = (total - hi.astype(jnp.float32)).astype(jnp.bfloat16)
        share_columns(w, 2 * k, WS, jnp.concatenate([hi, lo], axis=0))

    drain(send.at[CS], irec.at[0:n_tok - 1])
    sent_projection()
    reduce_image(2 * k)
    sent_columns(w, 2 * k, WS)

    def advance(step, carry):
        send_centred()
        sent_image()

        @on_core(1)
        def _():
            inv = inverse_factor()
            share_columns(w, k, WS, normalised(inv).astype(jnp.bfloat16))

        sent_projection()
        sent_gram()
        reduce_image(k)
        sent_columns(w, k, WS)
        return carry

    lax.fori_loop(1, ITERS, advance, 0)
    send_centred()
    sent_image()

    @on_core(1)
    def _():
        inv = inverse_factor()
        ibuf[...] = inv
        push(ibuf, ibuf, BS, tok, cx * CORES)
        projected = normalised(inv)
        share_columns(sbuf, 1, SS, jnp.mean(projected * projected, axis=0, keepdims=True))

    @on_core(0)
    def _():
        drain(recv.at[BS], ibuf)

    basis[...] = jnp.dot(ibuf[:, 0:k], x[...], precision=HIGHEST, preferred_element_type=jnp.float32)
    sent_projection()
    sent_gram()

    @on_core(1)
    def _():
        drain(send.at[BS], ibuf)

    sent_columns(sbuf, 1, SS)
    await_columns(sbuf, 1, SS)
    scores[...] = sbuf[...]


def finish(scores, basis, scores_out, basis_out):
    scores_out[...] = scores[0]
    basis_out[...] = basis[...]


def solution(mesh):
    n_tok, n_feat = mesh.shape["tok"], mesh.shape["feat"]
    nz, nx = n_tok // NY, n_feat // CORES

    def on_device(activations, start_basis):
        rows, cols = activations.shape
        k = start_basis.shape[0]
        vmem = pl.BlockSpec(memory_space=pltpu.VMEM)
        scores, basis = pl.pallas_call(
            functools.partial(kernel, nz, nx),
            out_shape=(jax.ShapeDtypeStruct((1, rows), jnp.float32), jax.ShapeDtypeStruct((k, cols), jnp.float32)),
            in_specs=[pl.BlockSpec(memory_space=pl.ANY)] * 2,
            out_specs=(vmem, vmem),
            scratch_shapes=[
                pltpu.VMEM((rows, cols), jnp.bfloat16),
                pltpu.VMEM((k, cols), jnp.float32),
                pltpu.VMEM((2 * k, cols), jnp.bfloat16),
                pltpu.VMEM((nx, k, rows // nx), jnp.float32),
                pltpu.VMEM((n_feat, k, rows // nx), jnp.float32),
                pltpu.VMEM((SUB, LANES), jnp.float32),
                pltpu.VMEM((n_feat, SUB, LANES), jnp.float32),
                pltpu.VMEM((2 * k, rows), jnp.bfloat16),
                pltpu.VMEM((k, cols), jnp.float32),
                pltpu.VMEM((n_tok, SUB, LANES), jnp.float32),
                pltpu.VMEM((1, SUB, LANES), jnp.float32),
                pltpu.VMEM((n_tok, SUB, LANES), jnp.float32),
                pltpu.VMEM((SUB, LANES), jnp.float32),
                pltpu.VMEM((1, rows), jnp.float32),
                pltpu.VMEM((k, LANES), jnp.float32),
                pltpu.SemaphoreType.DMA((2,)),
                pltpu.SemaphoreType.DMA((8,)),
                pltpu.SemaphoreType.DMA((8,)),
                pltpu.SemaphoreType.DMA((nx,)),
            ],
            compiler_params=pltpu.CompilerParams(collective_id=0, has_side_effects=True),
        )(activations, start_basis)
        return pl.pallas_call(
            finish,
            out_shape=(jax.ShapeDtypeStruct((rows,), jnp.float32), jax.ShapeDtypeStruct((k, cols), jnp.float32)),
            in_specs=[vmem, vmem],
            out_specs=(vmem, vmem),
        )(scores, basis)

    return jax.shard_map(
        on_device, mesh=mesh, in_specs=(P("tok", "feat"), P(None, "feat")),
        out_specs=(P("tok"), P(None, "feat")), check_vma=False,
    )
```

```python
import functools

import jax
import jax.numpy as jnp
from jax import lax
from jax.experimental import pallas as pl
from jax.experimental.pallas import tpu as pltpu
from jax.sharding import PartitionSpec as P

ITERS = 4
NY = 4
CORES = 2
LANES = 128
SUB = 8
MESH = pl.DeviceIdType.MESH
HIGHEST = lax.Precision.HIGHEST
NT = (((1,), (1,)), ((), ()))


def far_first(n):
    return sorted(range(n), key=lambda d: -min(d, n - d))


def tree_sum(terms):
    terms = list(terms)
    while len(terms) > 1:
        terms = [sum(terms[i + 1:i + 2], terms[i]) for i in range(0, len(terms), 2)]
    return terms[0]


def wide(v):
    return jnp.broadcast_to(v, (SUB, LANES))


def kernel(nz, nx, acts, start, scores, basis, a, x, xb, pbuf, prec, gbuf, grec, w, img, irec, own, crec, mean,
           sbuf, ibuf, a_sem, send, recv, precv):
    tok, feat = lax.axis_index("tok"), lax.axis_index("feat")
    n_tok, n_feat = nz * NY, nx * CORES
    z, y = tok // NY, tok % NY
    cx, core = feat // CORES, feat % CORES
    owner = cx * CORES + 1
    k = x.shape[0]
    rows = a.shape[0]
    width = rows // nx
    mine = pl.ds(pl.multiple_of(cx * width, LANES), width)
    PS, GS, WS, IS, XS, CS, SS, BS = range(8)

    tok_offsets = sorted(((dz, dy) for dz in range(nz) for dy in range(NY) if (dz, dy) != (0, 0)),
                         key=lambda o: -min(o[0], nz - o[0]) - min(o[1], NY - o[1]))

    def tok_peer(dz, dy):
        return lax.rem(z + dz, nz) * NY + lax.rem(y + dy, NY)

    def chip(dx):
        return lax.rem(cx + dx, nx)

    def push(src, dst, which, t, f, arrived=None):
        pltpu.make_async_remote_copy(
            src_ref=src, dst_ref=dst, send_sem=send.at[which],
            recv_sem=recv.at[which] if arrived is None else arrived,
            device_id=(t, f), device_id_type=MESH,
        ).start()

    def drain(sem, ref):
        pltpu.make_async_copy(ref, ref, sem).wait()

    def on_core(c):
        return pl.when(core == c)

    first = pltpu.make_async_copy(start, img, a_sem.at[0])
    first.start()
    load = pltpu.make_async_copy(acts, a, a_sem.at[1])
    load.start()
    barrier = pltpu.get_barrier_semaphore()

    def greet(t, f):
        pl.semaphore_signal(barrier, inc=1, device_id=(t, f), device_id_type=MESH)

    for dz, dy in tok_offsets:
        greet(tok_peer(dz, dy), feat)
    for dx in far_first(nx):
        greet(tok, chip(dx) * CORES + 1 - core)
        if dx:
            greet(tok, chip(dx) * CORES + core)

    lane = lax.broadcasted_iota(jnp.int32, (SUB, LANES), 1)
    sub = lax.broadcasted_iota(jnp.int32, (SUB, LANES), 0)

    def chunk(c):
        return slice(c * LANES, (c + 1) * LANES)

    def tile_at(ref, tz, ty):
        return ref.at[pl.ds(pl.multiple_of(ty * SUB, SUB), SUB), pl.ds(pl.multiple_of(tz * LANES, LANES), LANES)]

    def send_projection(r, shift):
        for dx in far_first(nx):
            to = chip(dx)
            block = a[pl.ds(pl.multiple_of(to * width, LANES), width), :]
            p = lax.dot_general(xb[0:r, :], block, NT, preferred_element_type=jnp.float32)
            if r > k:
                p = p[:k] + p[k:]
            if shift is not None:
                p = p - shift
            if shift is None:
                pbuf[dx] = p
                continue
            if dx:
                pbuf[dx] = p
                push(pbuf.at[dx], prec.at[dx * CORES + core], PS, tok, to * CORES + 1, precv.at[dx])
            else:
                @on_core(0)
                def _():
                    pbuf[0] = p
                    push(pbuf.at[0], prec.at[0], PS, tok, owner, precv.at[0])

                @on_core(1)
                def _():
                    prec[1] = p

    def sum_projection():
        drain(precv.at[0], prec.at[0])
        total = prec[0] + prec[1]
        for dx in reversed(far_first(nx)[:-1]):
            drain(precv.at[dx], prec.at[0:CORES])
            total = total + (prec[dx * CORES] + prec[dx * CORES + 1])
        return total

    def sent_projection():
        @on_core(0)
        def _():
            drain(send.at[PS], pbuf)

        @on_core(1)
        def _():
            drain(send.at[PS], pbuf.at[1:])

    def share_columns(ref, r, which, value):
        part = ref.at[0:r, mine]
        part[...] = value
        for dx in far_first(nx):
            push(part, part, which, tok, chip(dx) * CORES)
            if dx:
                push(part, part, which, tok, chip(dx) * CORES + 1)

    def await_columns(ref, r, which):
        @on_core(0)
        def _():
            drain(recv.at[which], ref.at[0:r])

        @on_core(1)
        def _():
            drain(recv.at[which], ref.at[0:r, 0:rows - width])

    def sent_columns(ref, r, which):
        @on_core(1)
        def _():
            drain(send.at[which], ref.at[0:r])
            drain(send.at[which], ref.at[0:r, 0:rows - width])

    def send_gram():
        both = xb[...]
        s = lax.dot_general(both, jnp.concatenate([both, both], axis=0), NT, preferred_element_type=jnp.float32)
        s = s[:k] + s[k:]
        packed = jnp.zeros((SUB, LANES), jnp.float32)
        for g in range(k // SUB):
            part = s[g * SUB:(g + 1) * SUB]
            part = jnp.where(lane < k, part + pltpu.roll(part, LANES - k, 1), 0.0)
            packed = packed + (pltpu.roll(part, g * k, 1) if g else part)
        gbuf[...] = packed
        for dx in far_first(nx)[:-1]:
            push(gbuf, grec.at[feat], GS, tok, chip(dx) * CORES + 1)

        @on_core(0)
        def _():
            push(gbuf, grec.at[feat], GS, tok, owner)

        @on_core(1)
        def _():
            grec[feat] = packed

    def sent_gram():
        for _ in range(nx - 1):
            drain(send.at[GS], gbuf)

        @on_core(0)
        def _():
            drain(send.at[GS], gbuf)

    def inverse_factor():
        drain(recv.at[GS], grec.at[0:n_feat - 1])
        packed = tree_sum(grec[s] for s in range(n_feat))
        groups = []
        for g in range(k // SUB):
            part = pltpu.roll(packed, LANES - g * k, 1) if g else packed
            groups.append(jnp.where(lane < k, part, jnp.where(lane - k == sub + g * SUB, 1.0, 0.0)))
        factor = []
        for b in range(k // SUB):
            column = [[wide(g[:, b * SUB + c:b * SUB + c + 1]) for g in groups[b:]] for c in range(SUB)]
            done = jnp.zeros((SUB, LANES), jnp.float32)
            for r in range(SUB):
                pivot = wide(column[r][0][r:r + 1, :])
                inverse = 1.0 / pivot
                pivot_row = wide(groups[b][r:r + 1, :])
                done = jnp.where(sub == r, pivot_row * lax.rsqrt(pivot), done)
                below = [jnp.where(sub > r, column[r][0], 0.0)] + column[r][1:]
                for c in range(r + 1, SUB):
                    scale = wide(column[c][0][r:r + 1, :]) * inverse
                    column[c] = [v - u * scale for v, u in zip(column[c], below)]
                scaled = pivot_row * inverse
                groups[b:] = [g - u * scaled for g, u in zip(groups[b:], below)]
            factor.append(pltpu.roll(done, LANES - k, 1))
        return jnp.concatenate(factor, axis=0)

    def split():
        v = x[...]
        hi = v.astype(jnp.bfloat16)
        hi32 = hi.astype(jnp.float32)
        lo = (v - hi32).astype(jnp.bfloat16)
        xb[0:k, :] = hi
        xb[k:, :] = lo
        return hi32 + lo.astype(jnp.float32)

    def send_centred():
        v = split()
        send_gram()
        acc = jnp.zeros((k, LANES), jnp.float32)
        for c in range(nz):
            acc = acc + v[:, chunk(c)] * mean[c:c + 1, :]
        send_projection(2 * k, jnp.sum(acc, axis=1, keepdims=True))

    def normalised(inv):
        return jnp.dot(inv[:, 0:k], sum_projection(), precision=HIGHEST, preferred_element_type=jnp.float32)

    def reduce_image(r):
        if r > k:
            drain(recv.at[CS], crec.at[0:n_tok - 1])
            mean[...] = tree_sum(crec[s] for s in range(n_tok)) / (n_tok * rows)
        await_columns(w, r, WS)
        weights = w[0:r, :]
        counts = jnp.sum(weights.astype(jnp.float32), axis=1, keepdims=True)
        if r > k:
            counts = counts[:k] + counts[k:]
        pairs = nz // 2
        for dg in far_first(pairs):
            g = lax.rem(z // 2 + dg, pairs)
            columns = pl.ds(pl.multiple_of(g * 2 * LANES, 2 * LANES), 2 * LANES)
            term = jnp.dot(weights, a[:, columns], preferred_element_type=jnp.float32)
            if r > k:
                term = term[:k] + term[k:]
            for e in range(2):
                tz = g * 2 + e
                tile_column = pl.ds(pl.multiple_of(tz * LANES, LANES), LANES)
                img[:, tile_column] = term[:, chunk(e)] - counts * mean[pl.ds(tz, 1), :]
            for dy in far_first(NY):
                ty = lax.rem(y + dy, NY)
                for e in range(1 if dg == 0 and dy == 0 else 0, 2):
                    tz = g * 2 + (lax.rem(z + e, 2) if dg == 0 else e)
                    push(tile_at(img, tz, ty), irec.at[tok], IS, tz * NY + ty, feat)
        irec[tok] = tile_at(img, z, y)[...]
        drain(recv.at[IS], irec.at[0:n_tok - 1])
        own[0] = tree_sum(irec[s] for s in range(n_tok))
        tile = tile_at(x, z, y)
        for dz, dy in tok_offsets:
            push(own.at[0], tile, XS, tok_peer(dz, dy), feat)
        tile[...] = own[0]
        drain(recv.at[XS], irec.at[0:n_tok - 1])

    def sent_image():
        drain(send.at[IS], irec.at[0:n_tok - 1])
        drain(send.at[XS], irec.at[0:n_tok - 1])

    first.wait()
    xb[0:k, :] = img[...].astype(jnp.bfloat16)
    load.wait()
    sums = jnp.dot(jnp.ones((SUB, rows), jnp.bfloat16), a[...], preferred_element_type=jnp.float32)
    packed_sums = jnp.zeros((SUB, LANES), jnp.float32)
    for c in range(nz):
        packed_sums = jnp.where(sub == c, sums[:, chunk(c)], packed_sums)
    gbuf[...] = packed_sums
    crec[tok] = packed_sums
    send_projection(k, None)
    pl.semaphore_wait(barrier, n_tok + n_feat - 2)
    for dx in far_first(nx)[:-1]:
        push(pbuf.at[dx], prec.at[dx * CORES + core], PS, tok, chip(dx) * CORES + 1, precv.at[dx])

    @on_core(0)
    def _():
        push(pbuf.at[0], prec.at[0], PS, tok, owner, precv.at[0])

    @on_core(1)
    def _():
        prec[1] = pbuf[0]

    for dz, dy in tok_offsets:
        push(gbuf, crec.at[tok], CS, tok_peer(dz, dy), feat)

    @on_core(1)
    def _():
        total = sum_projection()
        hi = total.astype(jnp.bfloat16)
        lo = (total - hi.astype(jnp.float32)).astype(jnp.bfloat16)
        share_columns(w, 2 * k, WS, jnp.concatenate([hi, lo], axis=0))

    drain(send.at[CS], irec.at[0:n_tok - 1])
    sent_projection()
    reduce_image(2 * k)
    sent_columns(w, 2 * k, WS)

    def advance(step, carry):
        send_centred()
        sent_image()

        @on_core(1)
        def _():
            inv = inverse_factor()
            share_columns(w, k, WS, normalised(inv).astype(jnp.bfloat16))

        sent_projection()
        sent_gram()
        reduce_image(k)
        sent_columns(w, k, WS)
        return carry

    lax.fori_loop(1, ITERS, advance, 0)
    send_centred()
    sent_image()

    @on_core(1)
    def _():
        inv = inverse_factor()
        ibuf[...] = inv
        push(ibuf, ibuf, BS, tok, cx * CORES)
        projected = normalised(inv)
        share_columns(sbuf, 1, SS, jnp.mean(projected * projected, axis=0, keepdims=True))

    @on_core(0)
    def _():
        drain(recv.at[BS], ibuf)

    img[...] = jnp.dot(ibuf[:, 0:k], x[...], precision=HIGHEST, preferred_element_type=jnp.float32)
    leave = pltpu.make_async_copy(img, basis, a_sem.at[0])
    leave.start()
    sent_projection()
    sent_gram()

    @on_core(1)
    def _():
        drain(send.at[BS], ibuf)

    sent_columns(sbuf, 1, SS)
    await_columns(sbuf, 1, SS)
    scores[...] = sbuf[...]
    leave.wait()


def finish(scores, basis, scores_out, basis_out):
    scores_out[...] = scores[0]
    basis_out[...] = basis[...]


def solution(mesh):
    n_tok, n_feat = mesh.shape["tok"], mesh.shape["feat"]
    nz, nx = n_tok // NY, n_feat // CORES

    def on_device(activations, start_basis):
        rows, cols = activations.shape
        k = start_basis.shape[0]
        vmem = pl.BlockSpec(memory_space=pltpu.VMEM)
        scores, basis = pl.pallas_call(
            functools.partial(kernel, nz, nx),
            out_shape=(jax.ShapeDtypeStruct((1, rows), jnp.float32), jax.ShapeDtypeStruct((k, cols), jnp.float32)),
            in_specs=[pl.BlockSpec(memory_space=pl.ANY)] * 2,
            out_specs=(vmem, pl.BlockSpec(memory_space=pl.ANY)),
            scratch_shapes=[
                pltpu.VMEM((rows, cols), jnp.bfloat16),
                pltpu.VMEM((k, cols), jnp.float32),
                pltpu.VMEM((2 * k, cols), jnp.bfloat16),
                pltpu.VMEM((nx, k, rows // nx), jnp.float32),
                pltpu.VMEM((n_feat, k, rows // nx), jnp.float32),
                pltpu.VMEM((SUB, LANES), jnp.float32),
                pltpu.VMEM((n_feat, SUB, LANES), jnp.float32),
                pltpu.VMEM((2 * k, rows), jnp.bfloat16),
                pltpu.VMEM((k, cols), jnp.float32),
                pltpu.VMEM((n_tok, SUB, LANES), jnp.float32),
                pltpu.VMEM((1, SUB, LANES), jnp.float32),
                pltpu.VMEM((n_tok, SUB, LANES), jnp.float32),
                pltpu.VMEM((SUB, LANES), jnp.float32),
                pltpu.VMEM((1, rows), jnp.float32),
                pltpu.VMEM((k, LANES), jnp.float32),
                pltpu.SemaphoreType.DMA((2,)),
                pltpu.SemaphoreType.DMA((8,)),
                pltpu.SemaphoreType.DMA((8,)),
                pltpu.SemaphoreType.DMA((nx,)),
            ],
            compiler_params=pltpu.CompilerParams(collective_id=0, has_side_effects=True),
        )(activations, start_basis)
        return pl.pallas_call(
            finish,
            out_shape=(jax.ShapeDtypeStruct((rows,), jnp.float32), jax.ShapeDtypeStruct((k, cols), jnp.float32)),
            in_specs=[vmem, vmem],
            out_specs=(vmem, vmem),
        )(scores, basis)

    return jax.shard_map(
        on_device, mesh=mesh, in_specs=(P("tok", "feat"), P(None, "feat")),
        out_specs=(P("tok"), P(None, "feat")), check_vma=False,
    )
```

```python
import functools

import jax
import jax.numpy as jnp
from jax import lax
from jax.experimental import pallas as pl
from jax.experimental.pallas import tpu as pltpu
from jax.sharding import PartitionSpec as P

ITERS = 4
NY = 4
CORES = 2
LANES = 128
SUB = 8
MESH = pl.DeviceIdType.MESH
HIGHEST = lax.Precision.HIGHEST
NT = (((1,), (1,)), ((), ()))


def far_first(n):
    return sorted(range(n), key=lambda d: -min(d, n - d))


def tree_sum(terms):
    terms = list(terms)
    while len(terms) > 1:
        terms = [sum(terms[i + 1:i + 2], terms[i]) for i in range(0, len(terms), 2)]
    return terms[0]


def wide(v):
    return jnp.broadcast_to(v, (SUB, LANES))


def kernel(nz, nx, acts, start, scores, basis, a, x, xb, pbuf, prec, gbuf, grec, w, img, irec, own, crec, mean,
           sbuf, ibuf, cbuf, tbuf, a_sem, send, recv, precv):
    tok, feat = lax.axis_index("tok"), lax.axis_index("feat")
    n_tok, n_feat = nz * NY, nx * CORES
    z, y = tok // NY, tok % NY
    cx, core = feat // CORES, feat % CORES
    owner = cx * CORES + 1
    k = x.shape[0]
    rows = a.shape[0]
    width = rows // nx
    mine = pl.ds(pl.multiple_of(cx * width, LANES), width)
    PS, GS, WS, IS, XS, CS, SS, BS = range(8)

    tok_offsets = sorted(((dz, dy) for dz in range(nz) for dy in range(NY) if (dz, dy) != (0, 0)),
                         key=lambda o: -min(o[0], nz - o[0]) - min(o[1], NY - o[1]))

    def tok_peer(dz, dy):
        return lax.rem(z + dz, nz) * NY + lax.rem(y + dy, NY)

    def chip(dx):
        return lax.rem(cx + dx, nx)

    def push(src, dst, which, t, f, arrived=None):
        pltpu.make_async_remote_copy(
            src_ref=src, dst_ref=dst, send_sem=send.at[which],
            recv_sem=recv.at[which] if arrived is None else arrived,
            device_id=(t, f), device_id_type=MESH,
        ).start()

    def drain(sem, ref):
        pltpu.make_async_copy(ref, ref, sem).wait()

    def on_core(c):
        return pl.when(core == c)

    first = pltpu.make_async_copy(start, img, a_sem.at[0])
    first.start()
    load = pltpu.make_async_copy(acts, a, a_sem.at[1])
    load.start()
    barrier = pltpu.get_barrier_semaphore()

    def greet(t, f):
        pl.semaphore_signal(barrier, inc=1, device_id=(t, f), device_id_type=MESH)

    for dz, dy in tok_offsets:
        greet(tok_peer(dz, dy), feat)
    for dx in far_first(nx):
        greet(tok, chip(dx) * CORES + 1 - core)
        if dx:
            greet(tok, chip(dx) * CORES + core)

    lane = lax.broadcasted_iota(jnp.int32, (SUB, LANES), 1)
    sub = lax.broadcasted_iota(jnp.int32, (SUB, LANES), 0)

    def chunk(c):
        return slice(c * LANES, (c + 1) * LANES)

    def tile_at(ref, tz, ty):
        return ref.at[pl.ds(pl.multiple_of(ty * SUB, SUB), SUB), pl.ds(pl.multiple_of(tz * LANES, LANES), LANES)]

    def send_projection(shift):
        for dx in far_first(nx):
            to = chip(dx)
            block = a[pl.ds(pl.multiple_of(to * width, LANES), width), :]
            p = lax.dot_general(xb[...], block, NT, preferred_element_type=jnp.float32)
            p = p[:k] + p[k:] - shift
            if dx:
                pbuf[dx] = p
                push(pbuf.at[dx], prec.at[dx * CORES + core], PS, tok, to * CORES + 1, precv.at[dx])
            else:
                @on_core(0)
                def _():
                    pbuf[0] = p
                    push(pbuf.at[0], prec.at[0], PS, tok, owner, precv.at[0])

                @on_core(1)
                def _():
                    prec[1] = p

    def compute_projection(shift):
        for dx in far_first(nx):
            to = chip(dx)
            block = a[pl.ds(pl.multiple_of(to * width, LANES), width), :]
            pbuf[dx] = lax.dot_general(xb[0:k, :], block, NT, preferred_element_type=jnp.float32) - shift

    def sum_projection():
        drain(precv.at[0], prec.at[0])
        total = prec[0] + prec[1]
        for dx in reversed(far_first(nx)[:-1]):
            drain(precv.at[dx], prec.at[0:CORES])
            total = total + (prec[dx * CORES] + prec[dx * CORES + 1])
        return total

    def sent_projection():
        @on_core(0)
        def _():
            drain(send.at[PS], pbuf)

        @on_core(1)
        def _():
            drain(send.at[PS], pbuf.at[1:])

    def share_columns(ref, r, which, value):
        part = ref.at[0:r, mine]
        part[...] = value
        for dx in far_first(nx):
            push(part, part, which, tok, chip(dx) * CORES)
            if dx:
                push(part, part, which, tok, chip(dx) * CORES + 1)

    def await_columns(ref, r, which):
        @on_core(0)
        def _():
            drain(recv.at[which], ref.at[0:r])

        @on_core(1)
        def _():
            drain(recv.at[which], ref.at[0:r, 0:rows - width])

    def sent_columns(ref, r, which):
        @on_core(1)
        def _():
            drain(send.at[which], ref.at[0:r])
            drain(send.at[which], ref.at[0:r, 0:rows - width])

    def send_gram():
        both = xb[...]
        s = lax.dot_general(both, jnp.concatenate([both, both], axis=0), NT, preferred_element_type=jnp.float32)
        s = s[:k] + s[k:]
        packed = jnp.zeros((SUB, LANES), jnp.float32)
        for g in range(k // SUB):
            part = s[g * SUB:(g + 1) * SUB]
            part = jnp.where(lane < k, part + pltpu.roll(part, LANES - k, 1), 0.0)
            packed = packed + (pltpu.roll(part, g * k, 1) if g else part)
        gbuf[...] = packed
        for dx in far_first(nx)[:-1]:
            push(gbuf, grec.at[feat], GS, tok, chip(dx) * CORES + 1)

        @on_core(0)
        def _():
            push(gbuf, grec.at[feat], GS, tok, owner)

        @on_core(1)
        def _():
            grec[feat] = packed

    def sent_gram():
        for _ in range(nx - 1):
            drain(send.at[GS], gbuf)

        @on_core(0)
        def _():
            drain(send.at[GS], gbuf)

    def inverse_factor():
        drain(recv.at[GS], grec.at[0:n_feat - 1])
        packed = tree_sum(grec[s] for s in range(n_feat))
        groups = []
        for g in range(k // SUB):
            part = pltpu.roll(packed, LANES - g * k, 1) if g else packed
            groups.append(jnp.where(lane < k, part, jnp.where(lane - k == sub + g * SUB, 1.0, 0.0)))
        factor = []
        for b in range(k // SUB):
            column = [[wide(g[:, b * SUB + c:b * SUB + c + 1]) for g in groups[b:]] for c in range(SUB)]
            done = jnp.zeros((SUB, LANES), jnp.float32)
            for r in range(SUB):
                pivot = wide(column[r][0][r:r + 1, :])
                inverse = 1.0 / pivot
                pivot_row = wide(groups[b][r:r + 1, :])
                done = jnp.where(sub == r, pivot_row * lax.rsqrt(pivot), done)
                below = [jnp.where(sub > r, column[r][0], 0.0)] + column[r][1:]
                for c in range(r + 1, SUB):
                    scale = wide(column[c][0][r:r + 1, :]) * inverse
                    column[c] = [v - u * scale for v, u in zip(column[c], below)]
                scaled = pivot_row * inverse
                groups[b:] = [g - u * scaled for g, u in zip(groups[b:], below)]
            factor.append(pltpu.roll(done, LANES - k, 1))
        return jnp.concatenate(factor, axis=0)

    def split():
        v = x[...]
        hi = v.astype(jnp.bfloat16)
        hi32 = hi.astype(jnp.float32)
        lo = (v - hi32).astype(jnp.bfloat16)
        xb[0:k, :] = hi
        xb[k:, :] = lo
        return hi32 + lo.astype(jnp.float32)

    def send_centred():
        v = split()
        send_gram()
        acc = jnp.zeros((k, LANES), jnp.float32)
        for c in range(nz):
            acc = acc + v[:, chunk(c)] * mean[c:c + 1, :]
        send_projection(jnp.sum(acc, axis=1, keepdims=True))

    def normalised(inv):
        return jnp.dot(inv[:, 0:k], sum_projection(), precision=HIGHEST, preferred_element_type=jnp.float32)

    def reduce_image(initial):
        if initial:
            drain(recv.at[CS], crec.at[0:n_tok - 1])
            mean[...] = tree_sum(crec[s] for s in range(n_tok)) / (n_tok * rows)
            packed = tbuf[...]
            taken = jnp.concatenate([packed[:, g:g + 1] for g in range(k // SUB)], axis=0)
            cbuf[...] = crec[tok] - mean[...] * rows
        await_columns(w, k, WS)
        weights = w[...]
        counts = jnp.sum(weights.astype(jnp.float32), axis=1, keepdims=True)
        pairs = nz // 2
        for dg in far_first(pairs):
            g = lax.rem(z // 2 + dg, pairs)
            columns = pl.ds(pl.multiple_of(g * 2 * LANES, 2 * LANES), 2 * LANES)
            term = jnp.dot(weights, a[:, columns], preferred_element_type=jnp.float32)
            for e in range(2):
                tz = g * 2 + e
                tile_column = pl.ds(pl.multiple_of(tz * LANES, LANES), LANES)
                part = term[:, chunk(e)] - counts * mean[pl.ds(tz, 1), :]
                if initial:
                    part = part + taken * cbuf[pl.ds(tz, 1), :]
                img[:, tile_column] = part
            for dy in far_first(NY):
                ty = lax.rem(y + dy, NY)
                for e in range(1 if dg == 0 and dy == 0 else 0, 2):
                    tz = g * 2 + (lax.rem(z + e, 2) if dg == 0 else e)
                    push(tile_at(img, tz, ty), irec.at[tok], IS, tz * NY + ty, feat)
        irec[tok] = tile_at(img, z, y)[...]
        drain(recv.at[IS], irec.at[0:n_tok - 1])
        own[0] = tree_sum(irec[s] for s in range(n_tok))
        tile = tile_at(x, z, y)
        for dz, dy in tok_offsets:
            push(own.at[0], tile, XS, tok_peer(dz, dy), feat)
        tile[...] = own[0]
        drain(recv.at[XS], irec.at[0:n_tok - 1])

    def sent_image():
        drain(send.at[IS], irec.at[0:n_tok - 1])
        drain(send.at[XS], irec.at[0:n_tok - 1])

    first.wait()
    xb[0:k, :] = img[...].astype(jnp.bfloat16)
    load.wait()
    sums = jnp.dot(jnp.ones((SUB, rows), jnp.bfloat16), a[...], preferred_element_type=jnp.float32)
    packed_sums = jnp.zeros((SUB, LANES), jnp.float32)
    for c in range(nz):
        packed_sums = jnp.where(sub == c, sums[:, chunk(c)], packed_sums)
    cbuf[...] = packed_sums
    crec[tok] = packed_sums
    v = xb[0:k, :].astype(jnp.float32)
    acc = jnp.zeros((k, LANES), jnp.float32)
    for c in range(nz):
        acc = acc + v[:, chunk(c)] * packed_sums[c:c + 1, :]
    shift = jnp.sum(acc, axis=1, keepdims=True) / rows
    packed = jnp.zeros((SUB, LANES), jnp.float32)
    for g in range(k // SUB):
        packed = jnp.where(lane == g, shift[g * SUB:(g + 1) * SUB], packed)
    gbuf[...] = packed
    grec[feat] = packed
    compute_projection(shift)
    pl.semaphore_wait(barrier, n_tok + n_feat - 2)
    for dx in far_first(nx)[:-1]:
        push(pbuf.at[dx], prec.at[dx * CORES + core], PS, tok, chip(dx) * CORES + 1, precv.at[dx])

    @on_core(0)
    def _():
        push(pbuf.at[0], prec.at[0], PS, tok, owner, precv.at[0])

    @on_core(1)
    def _():
        prec[1] = pbuf[0]

    for dx in far_first(nx):
        for c in range(CORES):
            if dx:
                push(gbuf, grec.at[feat], GS, tok, chip(dx) * CORES + c)
    push(gbuf, grec.at[feat], GS, tok, cx * CORES + 1 - core)
    for dz, dy in tok_offsets:
        push(cbuf, crec.at[tok], CS, tok_peer(dz, dy), feat)

    drain(recv.at[GS], grec.at[0:n_feat - 1])
    tbuf[...] = tree_sum(grec[s] for s in range(n_feat))

    @on_core(1)
    def _():
        share_columns(w, k, WS, sum_projection().astype(jnp.bfloat16))

    drain(send.at[CS], irec.at[0:n_tok - 1])
    sent_projection()
    for _ in range(n_feat - 1):
        drain(send.at[GS], gbuf)
    reduce_image(True)
    sent_columns(w, k, WS)

    def advance(step, carry):
        send_centred()
        sent_image()

        @on_core(1)
        def _():
            inv = inverse_factor()
            share_columns(w, k, WS, normalised(inv).astype(jnp.bfloat16))

        sent_projection()
        sent_gram()
        reduce_image(False)
        sent_columns(w, k, WS)
        return carry

    lax.fori_loop(1, ITERS, advance, 0)
    send_centred()
    sent_image()

    @on_core(1)
    def _():
        inv = inverse_factor()
        ibuf[...] = inv
        push(ibuf, ibuf, BS, tok, cx * CORES)
        projected = normalised(inv)
        share_columns(sbuf, 1, SS, jnp.mean(projected * projected, axis=0, keepdims=True))

    @on_core(0)
    def _():
        drain(recv.at[BS], ibuf)

    img[...] = jnp.dot(ibuf[:, 0:k], x[...], precision=HIGHEST, preferred_element_type=jnp.float32)
    leave = pltpu.make_async_copy(img, basis, a_sem.at[0])
    leave.start()
    sent_projection()
    sent_gram()

    @on_core(1)
    def _():
        drain(send.at[BS], ibuf)

    sent_columns(sbuf, 1, SS)
    await_columns(sbuf, 1, SS)
    scores[...] = sbuf[...]
    leave.wait()


def finish(scores, basis, scores_out, basis_out):
    scores_out[...] = scores[0]
    basis_out[...] = basis[...]


def solution(mesh):
    n_tok, n_feat = mesh.shape["tok"], mesh.shape["feat"]
    nz, nx = n_tok // NY, n_feat // CORES

    def on_device(activations, start_basis):
        rows, cols = activations.shape
        k = start_basis.shape[0]
        vmem = pl.BlockSpec(memory_space=pltpu.VMEM)
        scores, basis = pl.pallas_call(
            functools.partial(kernel, nz, nx),
            out_shape=(jax.ShapeDtypeStruct((1, rows), jnp.float32), jax.ShapeDtypeStruct((k, cols), jnp.float32)),
            in_specs=[pl.BlockSpec(memory_space=pl.ANY)] * 2,
            out_specs=(vmem, pl.BlockSpec(memory_space=pl.ANY)),
            scratch_shapes=[
                pltpu.VMEM((rows, cols), jnp.bfloat16),
                pltpu.VMEM((k, cols), jnp.float32),
                pltpu.VMEM((2 * k, cols), jnp.bfloat16),
                pltpu.VMEM((nx, k, rows // nx), jnp.float32),
                pltpu.VMEM((n_feat, k, rows // nx), jnp.float32),
                pltpu.VMEM((SUB, LANES), jnp.float32),
                pltpu.VMEM((n_feat, SUB, LANES), jnp.float32),
                pltpu.VMEM((k, rows), jnp.bfloat16),
                pltpu.VMEM((k, cols), jnp.float32),
                pltpu.VMEM((n_tok, SUB, LANES), jnp.float32),
                pltpu.VMEM((1, SUB, LANES), jnp.float32),
                pltpu.VMEM((n_tok, SUB, LANES), jnp.float32),
                pltpu.VMEM((SUB, LANES), jnp.float32),
                pltpu.VMEM((1, rows), jnp.float32),
                pltpu.VMEM((k, LANES), jnp.float32),
                pltpu.VMEM((SUB, LANES), jnp.float32),
                pltpu.VMEM((SUB, LANES), jnp.float32),
                pltpu.SemaphoreType.DMA((2,)),
                pltpu.SemaphoreType.DMA((8,)),
                pltpu.SemaphoreType.DMA((8,)),
                pltpu.SemaphoreType.DMA((nx,)),
            ],
            compiler_params=pltpu.CompilerParams(collective_id=0, has_side_effects=True),
        )(activations, start_basis)
        return pl.pallas_call(
            finish,
            out_shape=(jax.ShapeDtypeStruct((rows,), jnp.float32), jax.ShapeDtypeStruct((k, cols), jnp.float32)),
            in_specs=[vmem, vmem],
            out_specs=(vmem, vmem),
        )(scores, basis)

    return jax.shard_map(
        on_device, mesh=mesh, in_specs=(P("tok", "feat"), P(None, "feat")),
        out_specs=(P("tok"), P(None, "feat")), check_vma=False,
    )
```
